32 devices in a mesh: dp: 16 (over z, x, core), feat: 2 (over y).
Axes of the slice: x: 2, y: 2, z: 4, core: 2. Of those that a mesh axis runs over, the one named last changes fastest.
Arguments:
- view_a: bfloat16 [2048, 4096], P('dp', 'feat'), may hold values from -24 to 24
- view_b: bfloat16 [2048, 4096], P('dp', 'feat'), may hold values from -24 to 24
Outputs:
- grad_a: bfloat16 [2048, 4096], P('dp', 'feat')
- grad_b: bfloat16 [2048, 4096], P('dp', 'feat')
- loss: float32 [], replicated
The draws below stay inside these ranges and needn't reach their ends.
All inputs are finite; a program needn't handle non-finite values.
Results may differ from the reference program's by a relative error of at most 0.0068.
Values may be sent and summed in bfloat16 or wider, within the bound.
No kernel may reach another device: no remote copies, remote signals or barrier semaphores. Data moves between devices by JAX's collectives and lax.ppermute only.
A program may use at most 64 MiB of HBM per device.

```python
import math
import jax
import jax.numpy as jnp
from jax import lax

F = 4096
SAMPLES = 2048


def draw_pair(key):
    factors = max(F // 32, 4)
    own = jax.random.normal(jax.random.fold_in(key, 101), (SAMPLES, F), jnp.float32)
    loads = jax.random.normal(jax.random.fold_in(key, 102), (SAMPLES, factors), jnp.float32)
    mixing = jax.random.normal(jax.random.fold_in(key, 103), (factors, F), jnp.float32) / math.sqrt(factors)
    shared = jnp.dot(loads, mixing, precision=lax.Precision.HIGHEST)
    core_a = math.sqrt(0.5) * own + math.sqrt(0.5) * shared
    coupling = jax.random.uniform(jax.random.fold_in(key, 104), (F,), jnp.float32, 0.6, 0.95)
    noise = jax.random.normal(jax.random.fold_in(key, 105), (SAMPLES, F), jnp.float32)
    core_b = coupling * core_a + jnp.sqrt(1.0 - coupling * coupling) * noise
    first = jnp.clip(core_a, -8.0, 8.0)
    second = jnp.clip(core_b, -8.0, 8.0)
    return (first, second)


def draw_view_a(key, part):
    return draw_pair(key)[0].astype(jnp.bfloat16)


def draw_view_b(key, part):
    return draw_pair(key)[1].astype(jnp.bfloat16)


def setup_inputs(seed: int = 0) -> dict:
    streams_of = jax.random.split(jax.random.key(seed), 3)
    return {
        "view_a": draw_view_a(jax.random.fold_in(streams_of[2], 71), 0),
        "view_b": draw_view_b(jax.random.fold_in(streams_of[2], 71), 0),
    }


EPS = 1e-05
LAMBDA = 0.0051

def normalize(view):
    values = view.astype(jnp.float32)
    center = lax.optimization_barrier(jnp.mean(values, axis=0))
    spread = lax.optimization_barrier(jnp.mean(values * values, axis=0)) - center * center
    inverse = lax.rsqrt(spread + EPS)
    return ((values - center) * inverse, inverse)

def backward(grad, normed, inverse):
    first = lax.optimization_barrier(jnp.mean(grad, axis=0))
    second = lax.optimization_barrier(jnp.mean(grad * normed, axis=0))
    return (inverse * (grad - first - normed * second)).astype(jnp.bfloat16)

def reference(view_a, view_b):
    normed_a, inverse_a = normalize(view_a)
    normed_b, inverse_b = normalize(view_b)
    a_half = normed_a.astype(jnp.bfloat16)
    b_half = normed_b.astype(jnp.bfloat16)
    corr_t = jnp.dot(b_half.T, a_half, preferred_element_type=jnp.float32) / SAMPLES
    unit = jnp.eye(F, dtype=jnp.float32)
    total = jnp.sum(unit * (1.0 - corr_t) ** 2) + LAMBDA * jnp.sum((1.0 - unit) * corr_t * corr_t)
    loss = total / F
    grad_t = (unit * (-2.0 * (1.0 - corr_t)) + (1.0 - unit) * (2.0 * LAMBDA) * corr_t).astype(jnp.bfloat16)
    grad_na = jnp.dot(b_half, grad_t, preferred_element_type=jnp.float32)
    grad_nb = jnp.dot(a_half, grad_t.T, preferred_element_type=jnp.float32)
    return (backward(grad_na, normed_a, inverse_a), backward(grad_nb, normed_b, inverse_b), loss)
```

```python
import jax
import jax.numpy as jnp
from jax import lax
from jax.experimental import pallas as pl
from jax.experimental.pallas import tpu as pltpu
from jax.sharding import PartitionSpec as P

EPS = 1e-05
LAMBDA = 0.0051


def ring_order(chips):
    rows = 1
    while rows * rows < chips:
        rows *= 2
    cols = chips // rows
    if cols == 1 or rows % 2 or rows * cols != chips:
        return list(range(chips))
    cycle = [r * cols for r in range(rows)]
    for i, r in enumerate(reversed(range(rows))):
        line = list(range(1, cols))
        cycle += [r * cols + c for c in (line if i % 2 == 0 else line[::-1])]
    return cycle


def butterfly(value, axis):
    size = lax.axis_size(axis)
    step = 1
    while step < size:
        other = lax.ppermute(value, axis, [(i, i ^ step) for i in range(size)])
        value = (value.astype(jnp.float32) + other.astype(jnp.float32)).astype(value.dtype)
        step *= 2
    return value


def gram_kernel(n, lhs_a, lhs_b, off_a, off_b, *refs):
    chunks_a, chunks_b, out = refs[:n], refs[n : 2 * n], refs[2 * n]
    rows = chunks_a[0].shape[0]
    for k, (lhs, off, chunks) in enumerate(((lhs_a, off_a, chunks_a), (lhs_b, off_b, chunks_b))):
        for c, chunk in enumerate(chunks):
            part = lax.dot_general(
                lhs[...], chunk[...], (((1,), (1,)), ((), ())), preferred_element_type=jnp.float32
            )
            out[k, :, c * rows : (c + 1) * rows] = (part - off[...]).astype(jnp.bfloat16)


def gram(lhs_a, lhs_b, off_a, off_b, chunks_a, chunks_b):
    n = len(chunks_a)
    rows = chunks_a[0].shape[0]
    return pl.pallas_call(
        lambda *refs: gram_kernel(n, *refs),
        out_shape=jax.ShapeDtypeStruct((2, lhs_a.shape[0], n * rows), jnp.bfloat16),
        name=f"gram{n}",
    )(lhs_a, lhs_b, off_a, off_b, *chunks_a, *chunks_b)


def apply_kernel(n, k_ref, acc_a, acc_b, row_in, *refs):
    chunks_a, chunks_b = refs[:n], refs[n : 2 * n]
    out_a, out_b, row_out = refs[2 * n :]
    rows = chunks_a[0].shape[0]
    ga = acc_a[...]
    gb = acc_b[...]
    for c in range(n):
        ka = k_ref[0, :, c * rows : (c + 1) * rows]
        kb = k_ref[1, :, c * rows : (c + 1) * rows]
        ga += jnp.dot(kb, chunks_a[c][...], preferred_element_type=jnp.float32)
        gb += jnp.dot(ka, chunks_b[c][...], preferred_element_type=jnp.float32)
    out_a[...] = ga
    out_b[...] = gb
    fa = k_ref[0].astype(jnp.float32)
    fb = k_ref[1].astype(jnp.float32)
    row_out[0] = row_in[0] + jnp.sum(fa, axis=1, keepdims=True)
    row_out[1] = row_in[1] + jnp.sum(fb, axis=1, keepdims=True)
    row_out[2] = row_in[2] + jnp.sum(fa * fb, axis=1, keepdims=True)


def apply(k, acc_a, acc_b, row, chunks_a, chunks_b):
    n = len(chunks_a)
    return pl.pallas_call(
        lambda *refs: apply_kernel(n, *refs),
        out_shape=(
            jax.ShapeDtypeStruct(acc_a.shape, jnp.float32),
            jax.ShapeDtypeStruct(acc_b.shape, jnp.float32),
            jax.ShapeDtypeStruct(row.shape, jnp.float32),
        ),
        input_output_aliases={1: 0, 2: 1, 3: 2},
        name=f"apply{n}",
    )(k, acc_a, acc_b, row, *chunks_a, *chunks_b)


def shards(view_a, view_b):
    rows, local = view_a.shape
    groups = lax.axis_size("dp")
    count = rows * groups
    features = local * lax.axis_size("feat")
    chips = groups // 2
    order = ring_order(chips)

    def ring(step):
        return [
            (order[k] * 2 + c, order[(k + step) % chips] * 2 + c) for k in range(chips) for c in range(2)
        ]

    def move(x, step):
        return lax.ppermute(x, "dp", ring(step))

    def mate(x):
        return lax.ppermute(x, "dp", [(i, i ^ 1) for i in range(groups)])

    steps = [([view_a, mate(view_a)], [view_b, mate(view_b)])]
    fwd = (view_a, view_b)
    bwd = (view_a, view_b)
    for _ in range(1, chips // 2):
        fwd = (move(fwd[0], 1), move(fwd[1], 1))
        bwd = (move(bwd[0], -1), move(bwd[1], -1))
        steps.append(
            (
                [fwd[0], mate(fwd[0]), bwd[0], mate(bwd[0])],
                [fwd[1], mate(fwd[1]), bwd[1], mate(bwd[1])],
            )
        )
    last_a = move(fwd[0], 1)
    last_b = move(bwd[1], -1)
    steps.append(([last_a, mate(last_a)], [last_b, mate(last_b)]))

    vals_a = view_a.astype(jnp.float32)
    vals_b = view_b.astype(jnp.float32)
    sums = butterfly(
        jnp.stack(
            [
                jnp.sum(vals_a, axis=0),
                jnp.sum(vals_a * vals_a, axis=0),
                jnp.sum(vals_b, axis=0),
                jnp.sum(vals_b * vals_b, axis=0),
                jnp.sum(vals_a * vals_b, axis=0),
            ]
        ),
        "dp",
    )
    means = sums / count
    center_a, center_b = means[0], means[2]
    inverse_a = lax.rsqrt(means[1] - center_a * center_a + EPS)
    inverse_b = lax.rsqrt(means[3] - center_b * center_b + EPS)
    corr = (means[4] - center_a * center_b) * inverse_a * inverse_b
    grad_diag = lax.reduce_precision(-2.0 * (1.0 - corr), 8, 7)
    diag = grad_diag - (2.0 * LAMBDA) * corr
    own_loss = butterfly(jnp.full((8, 128), jnp.sum((1.0 - corr) ** 2 - LAMBDA * corr * corr)), "feat")

    normed_a = (vals_a - center_a) * inverse_a
    normed_b = (vals_b - center_b) * inverse_b
    lhs_a = (normed_a * inverse_a).astype(jnp.bfloat16)
    lhs_b = (normed_b * inverse_b).astype(jnp.bfloat16)
    off_a = jnp.sum(lhs_a.astype(jnp.float32) * center_a, axis=1, keepdims=True)
    off_b = jnp.sum(lhs_b.astype(jnp.float32) * center_b, axis=1, keepdims=True)

    acc_a = jnp.zeros((rows, local), jnp.float32)
    acc_b = jnp.zeros((rows, local), jnp.float32)
    row = jnp.zeros((3, rows, 1), jnp.float32)
    for chunks_a, chunks_b in steps:
        k = butterfly(gram(lhs_a, lhs_b, off_a, off_b, chunks_a, chunks_b), "feat")
        acc_a, acc_b, row = apply(k, acc_a, acc_b, row, chunks_a, chunks_b)

    scale = 2.0 * LAMBDA / count
    half_a = lax.reduce_precision(normed_a, 8, 7)
    half_b = lax.reduce_precision(normed_b, 8, 7)
    grad_na = (scale * inverse_a) * (acc_a - row[1] * center_a) + half_b * diag
    grad_nb = (scale * inverse_b) * (acc_b - row[0] * center_b) + half_a * diag
    stats = butterfly(
        jnp.stack(
            [
                jnp.sum(grad_na, axis=0),
                jnp.sum(grad_na * normed_a, axis=0),
                jnp.sum(grad_nb, axis=0),
                jnp.sum(grad_nb * normed_b, axis=0),
                jnp.full((local,), jnp.sum(row[2])),
            ]
        ),
        "dp",
    )
    loss = (own_loss[0, 0] + stats[4, 0] * (LAMBDA / (count * count))) / features
    stats = stats / count
    grad_a = (inverse_a * (grad_na - stats[0] - normed_a * stats[1])).astype(jnp.bfloat16)
    grad_b = (inverse_b * (grad_nb - stats[2] - normed_b * stats[3])).astype(jnp.bfloat16)
    return (grad_a, grad_b, loss)


def solution(mesh):
    placed = (P("dp", "feat"), P("dp", "feat"))
    return jax.shard_map(
        shards,
        mesh=mesh,
        in_specs=placed,
        out_specs=(P("dp", "feat"), P("dp", "feat"), P()),
        check_vma=False,
    )
```

```python
import jax
import jax.numpy as jnp
from jax import lax
from jax.experimental import pallas as pl
from jax.experimental.pallas import tpu as pltpu
from jax.sharding import PartitionSpec as P

EPS = 1e-05
LAMBDA = 0.0051
LANES = 128


def ring_order(chips):
    rows = 1
    while rows * rows < chips:
        rows *= 2
    cols = chips // rows
    if cols == 1 or rows % 2 or rows * cols != chips:
        return list(range(chips))
    cycle = [r * cols for r in range(rows)]
    for i, r in enumerate(reversed(range(rows))):
        line = list(range(1, cols))
        cycle += [r * cols + c for c in (line if i % 2 == 0 else line[::-1])]
    return cycle


def exchange(value, axis, step):
    return lax.ppermute(value, axis, [(i, i ^ step) for i in range(lax.axis_size(axis))])


def butterfly(value, axis, until=None):
    size = lax.axis_size(axis) if until is None else until
    step = 1
    while step < size:
        other = exchange(value, axis, step)
        value = (value.astype(jnp.float32) + other.astype(jnp.float32)).astype(value.dtype)
        step *= 2
    return value


def call(body, outs, *args, name):
    vmem = pl.BlockSpec(memory_space=pltpu.VMEM)
    return pl.pallas_call(
        body,
        out_shape=tuple(jax.ShapeDtypeStruct(s, d) for s, d in outs),
        in_specs=[vmem] * len(args),
        out_specs=tuple([vmem] * len(outs)),
        name=name,
        compiler_params=pltpu.CompilerParams(vmem_limit_bytes=16 * 1024 * 1024),
    )(*args)


def total(x):
    return jnp.sum(x, axis=0, keepdims=True)


def sums_body(va, vb, out):
    a = va[...].astype(jnp.float32)
    b = vb[...].astype(jnp.float32)
    out[0:1, :] = total(a)
    out[1:2, :] = total(a * a)
    out[2:3, :] = total(b)
    out[3:4, :] = total(b * b)
    out[4:5, :] = total(a * b)
    out[5:8, :] = jnp.zeros((3, out.shape[1]), jnp.float32)


def prep_body(count, va, vb, mine, other, lhs_a, lhs_b, off, coef, loss):
    means = (mine[...] + other[...]) * (1.0 / count)
    center_a, center_b = means[0:1], means[2:3]
    inverse_a = lax.rsqrt(means[1:2] - center_a * center_a + EPS)
    inverse_b = lax.rsqrt(means[3:4] - center_b * center_b + EPS)
    corr = (means[4:5] - center_a * center_b) * inverse_a * inverse_b
    grad_diag = (-2.0 * (1.0 - corr)).astype(jnp.bfloat16).astype(jnp.float32)
    coef[0:1, :] = center_a
    coef[1:2, :] = inverse_a
    coef[2:3, :] = center_b
    coef[3:4, :] = inverse_b
    coef[4:5, :] = grad_diag - (2.0 * LAMBDA) * corr
    coef[5:8, :] = jnp.zeros((3, coef.shape[1]), jnp.float32)
    gap = 1.0 - corr
    loss[...] = jnp.broadcast_to(
        jnp.sum(gap * gap - LAMBDA * corr * corr, axis=1, keepdims=True), loss.shape
    )
    for k, (v, center, inverse, lhs) in enumerate(
        ((va, center_a, inverse_a, lhs_a), (vb, center_b, inverse_b, lhs_b))
    ):
        half = ((v[...].astype(jnp.float32) - center) * (inverse * inverse)).astype(jnp.bfloat16)
        lhs[...] = half
        off[k] = jnp.sum(half.astype(jnp.float32) * center, axis=1, keepdims=True)


def gram_body(n, lhs_a, lhs_b, off, *refs):
    out = refs[2 * n]
    rows = refs[0].shape[0]
    for k, lhs in enumerate((lhs_a, lhs_b)):
        for c in range(n):
            part = lax.dot_general(
                lhs[...], refs[k * n + c][...], (((1,), (1,)), ((), ())), preferred_element_type=jnp.float32
            )
            out[k, :, c * rows : (c + 1) * rows] = (part - off[k]).astype(jnp.bfloat16)


def gram(lhs_a, lhs_b, off, chunks_a, chunks_b):
    n = len(chunks_a)
    rows = chunks_a[0].shape[0]
    return call(
        lambda *refs: gram_body(n, *refs),
        [((2, lhs_a.shape[0], n * rows), jnp.bfloat16)],
        lhs_a, lhs_b, off, *chunks_a, *chunks_b,
        name=f"gram{n}",
    )[0]


def add_up(first, n, k_mine, k_other, old, chunks_a, chunks_b):
    rows = chunks_a[0].shape[0]
    k = (k_mine[...].astype(jnp.float32) + k_other[...].astype(jnp.float32)).astype(jnp.bfloat16)
    full = k.astype(jnp.float32)
    ga = gb = None
    for c in range(n):
        ka = k[0, :, c * rows : (c + 1) * rows]
        kb = k[1, :, c * rows : (c + 1) * rows]
        pa = jnp.dot(kb, chunks_a[c][...], preferred_element_type=jnp.float32)
        pb = jnp.dot(ka, chunks_b[c][...], preferred_element_type=jnp.float32)
        ga = pa if ga is None else ga + pa
        gb = pb if gb is None else gb + pb
    row_a = jnp.sum(full[0], axis=1, keepdims=True)
    row_b = jnp.sum(full[1], axis=1, keepdims=True)
    row_ab = jnp.sum(full[0] * full[1], axis=1, keepdims=True)
    if first:
        return ga, gb, row_a, row_b, row_ab
    acc_a, acc_b, row = old
    return acc_a[...] + ga, acc_b[...] + gb, row[0] + row_a, row[1] + row_b, row[2] + row_ab


def apply_body(first, n, *refs):
    k_mine, k_other = refs[:2]
    old = () if first else refs[2:5]
    base = 2 + len(old)
    chunks_a, chunks_b = refs[base : base + n], refs[base + n : base + 2 * n]
    out_a, out_b, row_out = refs[base + 2 * n :]
    ga, gb, row_a, row_b, row_ab = add_up(first, n, k_mine, k_other, old, chunks_a, chunks_b)
    out_a[...] = ga
    out_b[...] = gb
    row_out[0] = row_a
    row_out[1] = row_b
    row_out[2] = row_ab


def apply(k_mine, k_other, old, chunks_a, chunks_b):
    n = len(chunks_a)
    rows, local = chunks_a[0].shape
    first = not old
    return call(
        lambda *refs: apply_body(first, n, *refs),
        [((rows, local), jnp.float32), ((rows, local), jnp.float32), ((3, rows, 1), jnp.float32)],
        k_mine, k_other, *old, *chunks_a, *chunks_b,
        name=f"apply{n}",
    )


def last_body(n, count, *refs):
    k_mine, k_other = refs[:2]
    chunks_a, chunks_b = refs[5 : 5 + n], refs[5 + n : 5 + 2 * n]
    va, vb, coef, out_a, out_b, stats = refs[5 + 2 * n :]
    ga, gb, row_a, row_b, row_ab = add_up(False, n, k_mine, k_other, refs[2:5], chunks_a, chunks_b)
    center_a, inverse_a, center_b, inverse_b, diag = (coef[i : i + 1, :] for i in range(5))
    scale = 2.0 * LAMBDA / count
    local = va.shape[1]
    normed_a = (va[...].astype(jnp.float32) - center_a) * inverse_a
    normed_b = (vb[...].astype(jnp.float32) - center_b) * inverse_b
    half_a = normed_a.astype(jnp.bfloat16).astype(jnp.float32)
    half_b = normed_b.astype(jnp.bfloat16).astype(jnp.float32)
    grad_na = (scale * inverse_a) * (ga - row_b * center_a) + half_b * diag
    grad_nb = (scale * inverse_b) * (gb - row_a * center_b) + half_a * diag
    out_a[...] = grad_na
    out_b[...] = grad_nb
    stats[0:1, :local] = total(grad_na)
    stats[1:2, :local] = total(grad_na * normed_a)
    stats[2:3, :local] = total(grad_nb)
    stats[3:4, :local] = total(grad_nb * normed_b)
    stats[:, local:] = jnp.broadcast_to(total(row_ab), (4, LANES))


def last(count, k_mine, k_other, old, chunks_a, chunks_b, va, vb, coef):
    n = len(chunks_a)
    rows, local = va.shape
    return call(
        lambda *refs: last_body(n, count, *refs),
        [((rows, local), jnp.float32), ((rows, local), jnp.float32), ((4, local + LANES), jnp.float32)],
        k_mine, k_other, *old, *chunks_a, *chunks_b, va, vb, coef,
        name="last",
    )


def finish_body(count, features, na, nb, va, vb, coef, mine, other, own_loss, out_a, out_b, loss):
    local = va.shape[1]
    stats = (mine[...] + other[...]) * (1.0 / count)
    center_a, inverse_a, center_b, inverse_b = (coef[i : i + 1, :] for i in range(4))
    normed_a = (va[...].astype(jnp.float32) - center_a) * inverse_a
    normed_b = (vb[...].astype(jnp.float32) - center_b) * inverse_b
    mean_a, cross_a, mean_b, cross_b = (stats[i : i + 1, :local] for i in range(4))
    out_a[...] = (inverse_a * (na[...] - mean_a - normed_a * cross_a)).astype(jnp.bfloat16)
    out_b[...] = (inverse_b * (nb[...] - mean_b - normed_b * cross_b)).astype(jnp.bfloat16)
    loss[...] = (own_loss[...] + stats[0:1, local:] * (LAMBDA / count)) / features


def shards(view_a, view_b):
    rows, local = view_a.shape
    groups = lax.axis_size("dp")
    count = rows * groups
    feats = lax.axis_size("feat")
    features = local * feats
    chips = groups // 2
    order = ring_order(chips)

    def move(x, step):
        return lax.ppermute(
            x,
            "dp",
            [(order[k] * 2 + c, order[(k + step) % chips] * 2 + c) for k in range(chips) for c in range(2)],
        )

    def mate(x):
        return exchange(x, "dp", 1)

    steps = [([view_a, mate(view_a)], [view_b, mate(view_b)])]
    fwd = (view_a, view_b)
    bwd = (view_a, view_b)
    for _ in range(1, chips // 2):
        fwd = (move(fwd[0], 1), move(fwd[1], 1))
        bwd = (move(bwd[0], -1), move(bwd[1], -1))
        steps.append(
            (
                [fwd[0], mate(fwd[0]), bwd[0], mate(bwd[0])],
                [fwd[1], mate(fwd[1]), bwd[1], mate(bwd[1])],
            )
        )
    last_a = move(fwd[0], 1)
    last_b = move(bwd[1], -1)
    steps.append(([last_a, mate(last_a)], [last_b, mate(last_b)]))

    sums = call(sums_body, [((8, local), jnp.float32)], view_a, view_b, name="sums")[0]
    sums = butterfly(sums, "dp", groups // 2)
    lhs_a, lhs_b, off, coef, own_loss = call(
        lambda *refs: prep_body(count, *refs),
        [
            ((rows, local), jnp.bfloat16),
            ((rows, local), jnp.bfloat16),
            ((2, rows, 1), jnp.float32),
            ((8, local), jnp.float32),
            ((1, LANES), jnp.float32),
        ],
        view_a, view_b, sums, exchange(sums, "dp", groups // 2),
        name="prep",
    )
    own_loss = butterfly(own_loss, "feat")

    old = ()
    for i, (chunks_a, chunks_b) in enumerate(steps):
        k = butterfly(gram(lhs_a, lhs_b, off, chunks_a, chunks_b), "feat", feats // 2)
        k_other = exchange(k, "feat", feats // 2)
        if i + 1 < len(steps):
            old = apply(k, k_other, old, chunks_a, chunks_b)
        else:
            na, nb, stats = last(count, k, k_other, old, chunks_a, chunks_b, view_a, view_b, coef)

    stats = butterfly(stats, "dp", groups // 2)
    grad_a, grad_b, loss = call(
        lambda *refs: finish_body(count, features, *refs),
        [((rows, local), jnp.bfloat16), ((rows, local), jnp.bfloat16), ((1, LANES), jnp.float32)],
        na, nb, view_a, view_b, coef, stats, exchange(stats, "dp", groups // 2), own_loss,
        name="finish",
    )
    return (grad_a, grad_b, loss[0, 0])


def solution(mesh):
    placed = (P("dp", "feat"), P("dp", "feat"))
    return jax.shard_map(
        shards,
        mesh=mesh,
        in_specs=placed,
        out_specs=(P("dp", "feat"), P("dp", "feat"), P()),
        check_vma=False,
    )
```
